128 devices in a mesh: slide: 2 (over z_lo), segment: 2 (over core), tile: 32 (over x, z_hi, y).
Axes of the slice: x: 4, y: 4, z: 4 (z_hi: 2, z_lo: 2; z = z_hi * 2 + z_lo), core: 2. Of those that a mesh axis runs over, the one named last changes fastest.
Arguments:
- images: bfloat16 [2, 64, 64, 4096], P('slide', 'tile'), may hold values from -6 to 6
- adjacency: int32 [2, 64, 8], P('slide', 'tile'), may hold values from -1 to 63, as said below
- conv_weight: bfloat16 [576, 64], replicated, may hold values from -0.25 to 0.25
- mix_weight: bfloat16 [64, 256], replicated, may hold values from -0.75 to 0.75
- skip_weight: bfloat16 [64, 256], replicated, may hold values from -0.75 to 0.75
- next_weight: bfloat16 [256, 512], replicated, may hold values from -0.375 to 0.375
- cotangent: bfloat16 [2, 64, 32, 16384], P('slide', 'tile'), may hold values from -0.015625 to 0.015625
Outputs:
- grad_conv: float32 [576, 64], replicated
- grad_mix: float32 [64, 256], replicated
- grad_skip: float32 [64, 256], replicated
- grad_next: float32 [256, 512], replicated
- tile_loss: float32 [2, 64], replicated
The draws below stay inside these ranges and needn't reach their ends.
Inputs may be any that keep to these rules, and one draw needn't show every extreme that they name: `adjacency`: tile t of a slide lies in row t // 2 of that slide's tile grid, which holds tiles 2 * (t // 2) onward in order from left to right; every neighbour lies in the same grid row or in the rows just before and after, and neighbours agree with one another's positions.
All inputs are finite; a program needn't handle non-finite values.
Results may differ from the reference program's by a relative error of at most 0.013.
Values may be sent and summed in bfloat16 or wider, within the bound.
No kernel may reach another device: no remote copies, remote signals or barrier semaphores. Data moves between devices by JAX's collectives and lax.ppermute only.
A program may use at most 128 MiB of HBM per device.

```python
import jax
import jax.numpy as jnp
from jax import lax

CH_IN = 64
CH_MID = 256
CH_OUT = 512
PIX = 64
TILE_DEV = 2
TILES = 64
SLIDES = 2


def draw_adjacency(key, part):
    grid_rows = TILES // TILE_DEV
    offsets = jax.random.randint(jax.random.fold_in(key, 7), (SLIDES, grid_rows), 0, TILE_DEV // 2 + 1).astype(jnp.int32)
    columns = jnp.arange(TILE_DEV, dtype=jnp.int32)
    row_ids = jnp.arange(grid_rows, dtype=jnp.int32)
    moves = [(-1, -1), (-1, 0), (-1, 1), (0, -1), (0, 1), (1, -1), (1, 0), (1, 1)]
    found = []
    for move in moves:
        other_row = row_ids + move[0]
        row_ok = (other_row >= 0) & (other_row < grid_rows)
        safe_row = jnp.clip(other_row, 0, grid_rows - 1)
        canvas = offsets[:, :, None] + columns[None, None, :] + move[1]
        other_col = canvas - offsets[:, safe_row][:, :, None]
        valid = row_ok[None, :, None] & (other_col >= 0) & (other_col < TILE_DEV)
        found.append(jnp.where(valid, safe_row[None, :, None] * TILE_DEV + other_col, -1))
    return jnp.stack(found, axis=-1).reshape(SLIDES, TILES, 8).astype(jnp.int32)


def level_of(key, shape, cuts, low, top_value):
    loudness = 1.0
    for dim, blocks in cuts:
        steps = jax.random.uniform(jax.random.fold_in(jax.random.fold_in(key, 6), dim), (blocks,), jnp.float32, low / len(cuts), top_value / len(cuts))
        loudness = loudness * jnp.repeat(jnp.exp(steps), shape[dim] // blocks).reshape((-1,) + (1,) * (len(shape) - 1 - dim))
    return loudness


def centred(rng, shape, deviation, limit, shards=(), held_as=jnp.bfloat16):
    entries = deviation * jax.random.normal(rng, shape, jnp.float32)
    if shards:
        entries = entries * level_of(rng, shape, shards, -0.22, 0.18)
    return jnp.clip(entries, -limit, limit).astype(held_as)


def setup_inputs(seed: int = 0) -> dict:
    streams_of = jax.random.split(jax.random.key(seed), 8)
    return {
        "images": centred(streams_of[0], (SLIDES, TILES, PIX, PIX * CH_IN), 1.0, 6.0, ((0, 2), (1, 32))),
        "adjacency": draw_adjacency(jax.random.fold_in(streams_of[7], 71), 0),
        "conv_weight": centred(streams_of[2], (9 * CH_IN, CH_IN), (9 * CH_IN) ** -0.5, 0.25),
        "mix_weight": centred(streams_of[3], (CH_IN, CH_MID), CH_IN ** -0.5, 0.75),
        "skip_weight": centred(streams_of[4], (CH_IN, CH_MID), CH_IN ** -0.5, 0.75),
        "next_weight": centred(streams_of[5], (CH_MID, CH_OUT), CH_MID ** -0.5, 0.375),
        "cotangent": centred(streams_of[6], (SLIDES, TILES, PIX // 2, PIX // 2 * CH_OUT), ((SLIDES * TILES * PIX * PIX // 4) ** -0.5), 0.015625, ((0, 2), (1, 32))),
    }


def slope(values):
    sig = jax.nn.sigmoid(values)
    return sig * (1.0 + values * (1.0 - sig))


def edge_strips(tile_maps):
    return jnp.stack([tile_maps[:, 0], tile_maps[:, -1], tile_maps[:, :, 0], tile_maps[:, :, -1]], axis=1)


def padded_tiles(tile_maps, strips, neighbours):
    present = neighbours >= 0
    safe_index = jnp.clip(neighbours, 0, strips.shape[0] - 1)

    def pick(slot, side):
        piece = strips[safe_index[:, slot], side]
        return piece * present[:, slot, None, None].astype(piece.dtype)

    north = pick(1, 1)
    south = pick(6, 0)
    west = pick(3, 3)
    east = pick(4, 2)
    corner_nw = pick(0, 1)[:, -1]
    corner_ne = pick(2, 1)[:, 0]
    corner_sw = pick(5, 0)[:, -1]
    corner_se = pick(7, 0)[:, 0]
    top_row = jnp.concatenate([corner_nw[:, None], north, corner_ne[:, None]], axis=1)
    low_row = jnp.concatenate([corner_sw[:, None], south, corner_se[:, None]], axis=1)
    middle = jnp.concatenate([west[:, :, None], tile_maps, east[:, :, None]], axis=2)
    return jnp.concatenate([top_row[:, None], middle, low_row[:, None]], axis=1)


def forward_first(padded, tile_maps, conv_weight, mix_weight, skip_weight):
    count = tile_maps.shape[0]
    pre_act = jnp.zeros((count * PIX * PIX, CH_IN), jnp.float32)
    for offset in range(9):
        patch = padded[:, offset // 3:offset // 3 + PIX, offset % 3:offset % 3 + PIX].reshape(-1, CH_IN)
        pre_act = pre_act + jnp.dot(patch, conv_weight[offset * CH_IN:(offset + 1) * CH_IN], preferred_element_type=jnp.float32)
    hidden = jax.nn.silu(pre_act).astype(jnp.bfloat16)
    summed = jnp.dot(hidden, mix_weight, preferred_element_type=jnp.float32) + jnp.dot(tile_maps.reshape(-1, CH_IN), skip_weight, preferred_element_type=jnp.float32)
    active = jax.nn.silu(summed).astype(jnp.bfloat16)
    return pre_act, hidden, summed, active


def pool_pairs(active, count):
    blocks = active.astype(jnp.float32).reshape(count, PIX // 2, 2, PIX // 2, 2, CH_MID)
    return jnp.mean(blocks, axis=(2, 4)).reshape(-1, CH_MID).astype(jnp.bfloat16)


def second_section(pooled, cotangent_rows, next_weight, count):
    logits = jnp.dot(pooled, next_weight, preferred_element_type=jnp.float32)
    target = cotangent_rows.astype(jnp.float32)
    tile_loss = jnp.sum((jax.nn.silu(logits) * target).reshape(count, -1), axis=1)
    grad_out = (target * slope(logits)).astype(jnp.bfloat16)
    grad_next = jnp.dot(pooled.T, grad_out, preferred_element_type=jnp.float32)
    grad_pooled = jnp.dot(grad_out, next_weight.T, preferred_element_type=jnp.float32).astype(jnp.bfloat16)
    return tile_loss, grad_next, grad_pooled


def backward_first(grad_pooled, padded, tile_maps, pre_act, hidden, summed, mix_weight, count):
    quarter = (grad_pooled.astype(jnp.float32) * 0.25).reshape(count, PIX // 2, 1, PIX // 2, 1, CH_MID)
    spread = jnp.broadcast_to(quarter, (count, PIX // 2, 2, PIX // 2, 2, CH_MID)).reshape(-1, CH_MID)
    grad_sum = (spread * slope(summed)).astype(jnp.bfloat16)
    grad_mix = jnp.dot(hidden.T, grad_sum, preferred_element_type=jnp.float32)
    grad_skip = jnp.dot(tile_maps.reshape(-1, CH_IN).T, grad_sum, preferred_element_type=jnp.float32)
    back_pre = jnp.dot(grad_sum, mix_weight.T, preferred_element_type=jnp.float32)
    grad_pre = (back_pre * slope(pre_act)).astype(jnp.bfloat16)
    pieces = []
    for offset in range(9):
        patch = padded[:, offset // 3:offset // 3 + PIX, offset % 3:offset % 3 + PIX].reshape(-1, CH_IN)
        pieces.append(jnp.dot(patch.T, grad_pre, preferred_element_type=jnp.float32))
    return jnp.concatenate(pieces, axis=0), grad_mix, grad_skip


def reference(images, adjacency, conv_weight, mix_weight, skip_weight, next_weight, cotangent):
    totals = (jnp.zeros((9 * CH_IN, CH_IN), jnp.float32), jnp.zeros((CH_IN, CH_MID), jnp.float32),
              jnp.zeros((CH_IN, CH_MID), jnp.float32), jnp.zeros((CH_MID, CH_OUT), jnp.float32))
    losses = []
    for slide_index in range(SLIDES):
        tile_maps = images[slide_index].reshape(TILES, PIX, PIX, CH_IN)
        strips = edge_strips(tile_maps)
        slide_adjacency = adjacency[slide_index]
        slide_cotangent = cotangent[slide_index]

        def block_step(carry, block):
            start = (block * TILE_DEV).astype(jnp.int32)
            own_maps = lax.dynamic_slice_in_dim(tile_maps, start, TILE_DEV, 0)
            near = lax.dynamic_slice_in_dim(slide_adjacency, start, TILE_DEV, 0)
            target_rows = lax.dynamic_slice_in_dim(slide_cotangent, start, TILE_DEV, 0).reshape(-1, CH_OUT)
            padded = padded_tiles(own_maps, strips, near)
            pre_act, hidden, summed, active = forward_first(padded, own_maps, conv_weight, mix_weight, skip_weight)
            pooled = pool_pairs(active, TILE_DEV)
            tile_loss, grad_next, grad_pooled = second_section(pooled, target_rows, next_weight, TILE_DEV)
            grad_conv, grad_mix, grad_skip = backward_first(grad_pooled, padded, own_maps, pre_act, hidden, summed, mix_weight, TILE_DEV)
            carry = (carry[0] + grad_conv, carry[1] + grad_mix, carry[2] + grad_skip, carry[3] + grad_next)
            return carry, tile_loss

        totals, loss_rows = lax.scan(block_step, totals, jnp.arange(TILES // TILE_DEV, dtype=jnp.int32))
        losses.append(loss_rows.reshape(-1))
    return totals[0], totals[1], totals[2], totals[3], jnp.stack(losses)
```

```python
import functools

import jax
import jax.numpy as jnp
from jax import lax
from jax.experimental import pallas as pl
from jax.experimental.pallas import tpu as pltpu
from jax.sharding import PartitionSpec as P

CH_IN = 64
CH_MID = 256
CH_OUT = 512
PIX = 64
HALF = 32
LANES = 128
GROUPS = PIX * CH_IN // LANES
QUADS = 4
STEPS = PIX // (4 * QUADS)
ROWS = 1024
F32 = jnp.float32
BF16 = jnp.bfloat16


def dot_nn(a, b):
    return jnp.dot(a, b, preferred_element_type=F32)


def dot_tn(a, b):
    return lax.dot_general(a, b, (((0,), (0,)), ((), ())), preferred_element_type=F32)


def dot_nt(a, b):
    return lax.dot_general(a, b, (((1,), (1,)), ((), ())), preferred_element_type=F32)


def silu_and_slope(v):
    sig = 0.5 * jnp.tanh(0.5 * v) + 0.5
    out = v * sig
    return out, sig + out * (1.0 - sig)


def chain(lhs, target, wc, wms, wn):
    half = lhs.shape[0] // 2
    hid, slope_pre = silu_and_slope(dot_nn(lhs, wc))
    hid = hid.astype(BF16)
    pairs, slopes, pooled = [], [], []
    for h in range(2):
        x = lhs[:, 5 * LANES + h * LANES : 6 * LANES + h * LANES]
        hx = jnp.concatenate([hid[:, h * LANES : (h + 1) * LANES], x], axis=1)
        act, slope = silu_and_slope(dot_nn(hx, wms))
        act = act.astype(BF16).astype(F32)
        side = act[:, :CH_MID] + act[:, CH_MID:]
        pooled.append((0.25 * (side[:half] + side[half:])).astype(BF16))
        pairs.append(hx)
        slopes.append(slope)
    pooled = jnp.concatenate(pooled, axis=0)
    out, slope_out = silu_and_slope(dot_nn(pooled, wn))
    loss = jnp.sum(out * target, axis=0, keepdims=True)
    grad_out = (target * slope_out).astype(BF16)
    grad_next = dot_tn(pooled, grad_out)
    grad_pooled = dot_nt(grad_out, wn).astype(BF16).astype(F32) * 0.25
    grad_ms, back = None, []
    for h in range(2):
        g = grad_pooled[h * half : (h + 1) * half]
        g = jnp.concatenate([g, g], axis=0)
        g = jnp.concatenate([g, g], axis=1)
        grad_sum = (g * slopes[h]).astype(BF16)
        part = dot_tn(pairs[h], grad_sum)
        grad_ms = part if grad_ms is None else grad_ms + part
        back.append(dot_nt(grad_sum, wms[:LANES]))
    grad_pre = (jnp.concatenate(back, axis=1) * slope_pre).astype(BF16)
    return loss, grad_next, grad_ms, dot_tn(grad_pre, lhs)


def build_weights(conv_ref, mix_ref, skip_ref, wc, wms):
    zero = jnp.zeros((CH_IN, CH_IN), BF16)
    for r in range(3):
        for w in range(8):
            row = []
            for b in range(4):
                c = w - b - 1
                at = (3 * r + c) * CH_IN
                row.append(conv_ref[at : at + CH_IN, :] if 0 <= c <= 2 else zero)
            wc[r * 512 + w * CH_IN : r * 512 + (w + 1) * CH_IN, :] = jnp.concatenate(row, axis=1)
    wms[...] = jnp.zeros_like(wms)
    for k in range(2):
        wms[k * CH_IN : (k + 1) * CH_IN, k * CH_MID : (k + 1) * CH_MID] = mix_ref[...]
        wms[(2 + k) * CH_IN : (3 + k) * CH_IN, k * CH_MID : (k + 1) * CH_MID] = skip_ref[...]


def sums_of_taps(acc):
    taps = []
    for r in range(3):
        for c in range(3):
            parts = [None, None]
            for b in range(4):
                w = b + c + 1
                at = r * 512 + (w // 2) * LANES
                piece = acc[b * CH_IN : (b + 1) * CH_IN, at : at + LANES]
                parts[w % 2] = piece if parts[w % 2] is None else parts[w % 2] + piece
            taps.append(parts[0] + pltpu.roll(parts[1], CH_IN, 1))
    return taps


def pack(ids_ref, loss, gnext, gms, gconv, next_ref, rest_ref):
    for k in range(4):
        next_ref[k * 256 : (k + 1) * 256, :] = gnext[:, k * LANES : (k + 1) * LANES].astype(BF16)
    for k, tap in enumerate(sums_of_taps(gconv)):
        rest_ref[k * 64 : (k + 1) * 64, :] = tap.astype(BF16)
    for k in range(2):
        low, high = gms[2 * k * CH_IN : (2 * k + 1) * CH_IN, :CH_MID], gms[(2 * k + 1) * CH_IN : (2 * k + 2) * CH_IN, CH_MID:]
        both = (low + high).astype(BF16)
        for n in range(2):
            at = 576 + k * 128 + n * 64
            rest_ref[at : at + 64, :] = both[:, n * LANES : (n + 1) * LANES]
    total = jnp.sum(loss)
    lane = lax.broadcasted_iota(jnp.int32, (8, LANES), 1)
    value = jnp.where(lane == ids_ref[2], total, 0.0)
    upper = value.astype(BF16)
    rest_ref[832:840, :] = upper
    rest_ref[840:848, :] = (value - upper.astype(F32)).astype(BF16)
    rest_ref[848:ROWS, :] = jnp.zeros((ROWS - 848, LANES), BF16)


def tile_kernel(ids_ref, adj_ref, img_ref, west_ref, east_ref, north_ref, south_ref, cot_ref, conv_ref, mix_ref, skip_ref, wn_ref,
                keep_ref, send_ref, rows_f, xs, lhs, wc, wms, acc_loss, acc_next, acc_ms, acc_conv):
    step = pl.program_id(0)
    core = ids_ref[0]

    def known(slot):
        return (adj_ref[core * 8 + slot] >= 0).astype(F32)

    def local(slot, row):
        return jnp.clip(adj_ref[core * 8 + slot] - (ids_ref[1] + row) * 2, 0, 1)

    @pl.when(step == 0)
    def _():
        build_weights(conv_ref, mix_ref, skip_ref, wc, wms)
        acc_loss[...] = jnp.zeros_like(acc_loss)
        acc_next[...] = jnp.zeros_like(acc_next)
        acc_ms[...] = jnp.zeros_like(acc_ms)
        acc_conv[...] = jnp.zeros_like(acc_conv)
        for k in range(GROUPS):
            rows_f[k + 1, 8 : 8 + PIX, :] = img_ref[:, k * LANES : (k + 1) * LANES].astype(F32)
        rows_f[0, 8 : 8 + PIX, :] = west_ref[...].astype(F32) * known(3)
        rows_f[GROUPS + 1, 8 : 8 + PIX, :] = east_ref[...].astype(F32) * known(4)
        for ref, at, row, slots in ((north_ref, 7, -1, (0, 1, 2)), (south_ref, 8 + PIX, 1, (5, 6, 7))):
            both = ref[...].astype(F32)

            def picked(slot):
                return jnp.where(local(slot, row) == 0, both[0:1], both[1:2]) * known(slot)

            rows_f[0, at : at + 1, :] = picked(slots[0])[:, (GROUPS - 1) * LANES :]
            middle = picked(slots[1])
            for k in range(GROUPS):
                rows_f[k + 1, at : at + 1, :] = middle[:, k * LANES : (k + 1) * LANES]
            rows_f[GROUPS + 1, at : at + 1, :] = picked(slots[2])[:, :LANES]
        for k in range(GROUPS + 2):
            for n, first in enumerate((7, 8, 9, 10)):
                xs[n, k] = rows_f[k, pl.ds(first, HALF, stride=2), :].astype(BF16)

    for m in range(QUADS):
        group = 2 * (step * QUADS + m)
        for odd in range(2):
            at = (odd * QUADS + m) * HALF
            for r in range(3):
                for k in range(4):
                    lhs[at : at + HALF, r * 512 + k * LANES : r * 512 + (k + 1) * LANES] = xs[odd + r, group + k]
    target = jnp.concatenate(
        [cot_ref[:, (2 * m + h) * CH_OUT : (2 * m + h + 1) * CH_OUT] for h in range(2) for m in range(QUADS)], axis=0
    ).astype(F32)
    loss, gnext, gms, gconv = chain(lhs[...], target, wc[...], wms[...], wn_ref[...])
    acc_loss[...] += loss
    acc_next[...] += gnext
    acc_ms[...] += gms
    acc_conv[...] += gconv

    for number, first, second in ((0, keep_ref, send_ref), (1, send_ref, keep_ref)):
        @pl.when((step == STEPS - 1) & (core == number))
        def _(first=first, second=second):
            pack(ids_ref, acc_loss[...], acc_next[...], acc_ms[...], acc_conv, first, second)


def run_tile(ids, adjacency, images, north, south, cotangent, conv_weight, mix_weight, skip_weight, next_weight):
    def pair_of(slot):
        def index(step, ids_ref, adj_ref):
            near = adj_ref[ids_ref[0] * 8 + slot] - ids_ref[1] * 2
            return (0, jnp.clip(near, 0, 1), 0, GROUPS - 1 if slot == 3 else 0)

        return index

    def whole(shape):
        return pl.BlockSpec(shape, lambda step, ids_ref, adj_ref: (0,) * len(shape))

    return pl.pallas_call(
        tile_kernel,
        out_shape=[jax.ShapeDtypeStruct((ROWS, LANES), BF16)] * 2,
        grid_spec=pltpu.PrefetchScalarGridSpec(
            num_scalar_prefetch=2,
            grid=(STEPS,),
            in_specs=[
                pl.BlockSpec((None, None, PIX, PIX * CH_IN), lambda step, ids_ref, adj_ref: (0, ids_ref[0], 0, 0)),
                pl.BlockSpec((None, None, PIX, LANES), pair_of(3)),
                pl.BlockSpec((None, None, PIX, LANES), pair_of(4)),
                whole((2, PIX * CH_IN)),
                whole((2, PIX * CH_IN)),
                pl.BlockSpec((None, None, HALF, 2 * QUADS * CH_OUT), lambda step, ids_ref, adj_ref: (0, ids_ref[0], 0, step)),
                whole((9 * CH_IN, CH_IN)),
                whole((CH_IN, CH_MID)),
                whole((CH_IN, CH_MID)),
                whole((CH_MID, CH_OUT)),
            ],
            out_specs=[whole((ROWS, LANES))] * 2,
            scratch_shapes=[
                pltpu.VMEM((GROUPS + 2, 80, LANES), F32),
                pltpu.VMEM((4, GROUPS + 2, HALF, LANES), BF16),
                pltpu.VMEM((2 * QUADS * HALF, 1536), BF16),
                pltpu.VMEM((1536, 256), BF16),
                pltpu.VMEM((256, 512), BF16),
                pltpu.VMEM((1, CH_OUT), F32),
                pltpu.VMEM((CH_MID, CH_OUT), F32),
                pltpu.VMEM((256, 512), F32),
                pltpu.VMEM((256, 1536), F32),
            ],
        ),
        name="tile",
    )(ids, adjacency, images, images, images, north, south, cotangent, conv_weight, mix_weight, skip_weight, next_weight)


def unpack_kernel(ids_ref, own_ref, other_ref, conv_ref, mix_ref, skip_ref, next_ref, loss_ref):
    def unpack(wide_ref, rest_ref):
        for k in range(4):
            next_ref[:, k * LANES : (k + 1) * LANES] = wide_ref[k * 256 : (k + 1) * 256, :].astype(F32)
        for k in range(9):
            tap = rest_ref[k * 64 : (k + 1) * 64, :].astype(F32)
            conv_ref[k * CH_IN : (k + 1) * CH_IN, :] = tap.T[:CH_IN, :]
        for k, ref in enumerate((mix_ref, skip_ref)):
            for n in range(2):
                at = 576 + k * 128 + n * 64
                ref[:, n * LANES : (n + 1) * LANES] = rest_ref[at : at + 64, :].astype(F32)
        loss_ref[...] = rest_ref[832:840, :].astype(F32) + rest_ref[840:848, :].astype(F32)

    @pl.when(ids_ref[0] == 0)
    def _():
        unpack(own_ref, other_ref)

    @pl.when(ids_ref[0] != 0)
    def _():
        unpack(other_ref, own_ref)


def run_unpack(ids, own, other):
    return pl.pallas_call(
        unpack_kernel,
        out_shape=[
            jax.ShapeDtypeStruct((9 * CH_IN, CH_IN), F32),
            jax.ShapeDtypeStruct((CH_IN, CH_MID), F32),
            jax.ShapeDtypeStruct((CH_IN, CH_MID), F32),
            jax.ShapeDtypeStruct((CH_MID, CH_OUT), F32),
            jax.ShapeDtypeStruct((8, LANES), F32),
        ],
        in_specs=[pl.BlockSpec(memory_space=pltpu.SMEM), pl.BlockSpec(memory_space=pltpu.VMEM), pl.BlockSpec(memory_space=pltpu.VMEM)],
        out_specs=[pl.BlockSpec(memory_space=pltpu.VMEM)] * 5,
        name="unpack",
    )(ids, own, other)


def body(slides, rows, images, adjacency, conv_weight, mix_weight, skip_weight, next_weight, cotangent):
    core = lax.axis_index("segment").astype(jnp.int32)
    row = lax.axis_index("tile").astype(jnp.int32)
    place = lax.axis_index("slide").astype(jnp.int32) * (2 * rows) + row * 2 + core
    ids = jnp.stack([core, row, place])
    north = lax.ppermute(images[0, :, PIX - 1], "tile", [(i, i + 1) for i in range(rows - 1)])
    south = lax.ppermute(images[0, :, 0], "tile", [(i + 1, i) for i in range(rows - 1)])
    keep, send = run_tile(
        ids, adjacency.reshape(-1), images, north, south, cotangent, conv_weight, mix_weight, skip_weight, next_weight
    )
    swap = [(0, 1), (1, 0)]
    group = ("slide", "tile")
    parts = slides * rows
    got = lax.ppermute(send, "segment", swap)
    own = (keep.astype(F32) + got.astype(F32)).astype(BF16).reshape(parts, ROWS // parts, LANES)
    pieces = lax.all_to_all(own, group, 0, 0, tiled=True)
    total = jnp.sum(pieces.astype(F32), axis=0).astype(BF16)
    copies = jnp.broadcast_to(total[None], (parts, ROWS // parts, LANES))
    own = lax.all_to_all(copies, group, 0, 0, tiled=True).reshape(ROWS, LANES)
    other = lax.ppermute(own, "segment", swap)
    conv, mix, skip, nxt, loss = run_unpack(ids, own, other)
    return conv, mix, skip, nxt, loss[0, : slides * rows * 2].reshape(slides, 2 * rows)


def solution(mesh):
    placed = (
        P("slide", "tile", None, None),
        P("slide", "tile", None),
        P(),
        P(),
        P(),
        P(),
        P("slide", "tile", None, None),
    )
    return jax.shard_map(
        functools.partial(body, mesh.shape["slide"], mesh.shape["tile"]),
        mesh=mesh,
        in_specs=placed,
        out_specs=(P(), P(), P(), P(), P()),
        check_vma=False,
    )
```

```python
import functools

import jax
import jax.numpy as jnp
from jax import lax
from jax.experimental import pallas as pl
from jax.experimental.pallas import tpu as pltpu
from jax.sharding import PartitionSpec as P

CH_IN = 64
CH_MID = 256
CH_OUT = 512
PIX = 64
HALF = 32
LANES = 128
GROUPS = PIX * CH_IN // LANES
QUADS = 4
STEPS = PIX // (4 * QUADS)
ROWS = 1024
F32 = jnp.float32
BF16 = jnp.bfloat16


def dot_nn(a, b):
    return jnp.dot(a, b, preferred_element_type=F32)


def dot_tn(a, b):
    return lax.dot_general(a, b, (((0,), (0,)), ((), ())), preferred_element_type=F32)


def dot_nt(a, b):
    return lax.dot_general(a, b, (((1,), (1,)), ((), ())), preferred_element_type=F32)


def silu_and_slope(v):
    sig = 0.5 * jnp.tanh(0.5 * v) + 0.5
    out = v * sig
    return out, sig + out * (1.0 - sig)


def chain(lhs, target, wc, wms, wn):
    half = lhs.shape[0] // 2
    hid, slope_pre = silu_and_slope(dot_nn(lhs, wc))
    hid = hid.astype(BF16)
    pairs, slopes, pooled = [], [], []
    for h in range(2):
        x = lhs[:, 5 * LANES + h * LANES : 6 * LANES + h * LANES]
        hx = jnp.concatenate([hid[:, h * LANES : (h + 1) * LANES], x], axis=1)
        act, slope = silu_and_slope(dot_nn(hx, wms))
        act = act.astype(BF16).astype(F32)
        side = act[:, :CH_MID] + act[:, CH_MID:]
        pooled.append((0.25 * (side[:half] + side[half:])).astype(BF16))
        pairs.append(hx)
        slopes.append(slope)
    pooled = jnp.concatenate(pooled, axis=0)
    out, slope_out = silu_and_slope(dot_nn(pooled, wn))
    loss = jnp.sum(out * target, axis=0, keepdims=True)
    grad_out = (target * slope_out).astype(BF16)
    grad_next = dot_tn(pooled, grad_out)
    grad_pooled = dot_nt(grad_out, wn).astype(BF16).astype(F32) * 0.25
    grad_ms, back = None, []
    for h in range(2):
        g = grad_pooled[h * half : (h + 1) * half]
        g = jnp.concatenate([g, g], axis=0)
        g = jnp.concatenate([g, g], axis=1)
        grad_sum = (g * slopes[h]).astype(BF16)
        part = dot_tn(pairs[h], grad_sum)
        grad_ms = part if grad_ms is None else grad_ms + part
        back.append(dot_nt(grad_sum, wms[:LANES]))
    grad_pre = (jnp.concatenate(back, axis=1) * slope_pre).astype(BF16)
    return loss, grad_next, grad_ms, dot_tn(grad_pre, lhs)


def build_weights(conv_ref, mix_ref, skip_ref, wc, wms):
    zero = jnp.zeros((CH_IN, CH_IN), BF16)
    taps = []
    for k in range(9):
        if k % 2 == 0:
            wide = min(LANES, (9 - k) * CH_IN)
            pair = conv_ref[:, k * CH_IN : k * CH_IN + wide].astype(F32).T.astype(BF16)
        taps.append(pair[(k % 2) * CH_IN : (k % 2 + 1) * CH_IN, :])
    for r in range(3):
        for w in range(8):
            row = []
            for b in range(4):
                c = w - b - 1
                row.append(taps[3 * r + c] if 0 <= c <= 2 else zero)
            wc[r * 512 + w * CH_IN : r * 512 + (w + 1) * CH_IN, :] = jnp.concatenate(row, axis=1)
    wms[...] = jnp.zeros_like(wms)
    for k in range(2):
        wms[k * CH_IN : (k + 1) * CH_IN, k * CH_MID : (k + 1) * CH_MID] = mix_ref[...]
        wms[(2 + k) * CH_IN : (3 + k) * CH_IN, k * CH_MID : (k + 1) * CH_MID] = skip_ref[...]


def sums_of_taps(acc):
    taps = []
    for r in range(3):
        for c in range(3):
            parts = [None, None]
            for b in range(4):
                w = b + c + 1
                at = r * 512 + (w // 2) * LANES
                piece = acc[b * CH_IN : (b + 1) * CH_IN, at : at + LANES]
                parts[w % 2] = piece if parts[w % 2] is None else parts[w % 2] + piece
            taps.append(parts[0] + pltpu.roll(parts[1], CH_IN, 1))
    return taps


def pack(ids_ref, loss, gnext, gms, gconv, next_ref, rest_ref):
    for k in range(4):
        next_ref[k * 256 : (k + 1) * 256, :] = gnext[:, k * LANES : (k + 1) * LANES].astype(BF16)
    for k, tap in enumerate(sums_of_taps(gconv)):
        rest_ref[k * 64 : (k + 1) * 64, :] = tap.astype(BF16)
    for k in range(2):
        low, high = gms[2 * k * CH_IN : (2 * k + 1) * CH_IN, :CH_MID], gms[(2 * k + 1) * CH_IN : (2 * k + 2) * CH_IN, CH_MID:]
        both = (low + high).astype(BF16)
        for n in range(2):
            at = 576 + k * 128 + n * 64
            rest_ref[at : at + 64, :] = both[:, n * LANES : (n + 1) * LANES]
    total = jnp.sum(loss)
    lane = lax.broadcasted_iota(jnp.int32, (8, LANES), 1)
    value = jnp.where(lane == ids_ref[2], total, 0.0)
    upper = value.astype(BF16)
    rest_ref[832:840, :] = upper
    rest_ref[840:848, :] = (value - upper.astype(F32)).astype(BF16)
    rest_ref[848:ROWS, :] = jnp.zeros((ROWS - 848, LANES), BF16)


def tile_kernel(ids_ref, adj_ref, img_ref, west_ref, east_ref, inner_ref, outer_ref, cot_ref, conv_ref, mix_ref, skip_ref, wn_ref,
                keep_ref, send_ref, rows_f, xs, lhs, wc, wms, acc_loss, acc_next, acc_ms, acc_conv):
    step = pl.program_id(0)
    core = ids_ref[0]

    def known(slot):
        return (adj_ref[core, slot] >= 0).astype(F32)

    def local(slot, row):
        return jnp.clip(adj_ref[core, slot] - (ids_ref[1] + row) * 2, 0, 1)

    @pl.when(step == 0)
    def _():
        build_weights(conv_ref, mix_ref, skip_ref, wc, wms)
        acc_loss[...] = jnp.zeros_like(acc_loss)
        acc_next[...] = jnp.zeros_like(acc_next)
        acc_ms[...] = jnp.zeros_like(acc_ms)
        acc_conv[...] = jnp.zeros_like(acc_conv)
        for k in range(GROUPS):
            rows_f[k + 1, 8 : 8 + PIX, :] = img_ref[:, k * LANES : (k + 1) * LANES].astype(F32)
        rows_f[0, 8 : 8 + PIX, :] = west_ref[...].astype(F32) * known(3)
        rows_f[GROUPS + 1, 8 : 8 + PIX, :] = east_ref[...].astype(F32) * known(4)
        even = ids_ref[1] % 2 == 0
        inner, outer = inner_ref[...].astype(F32), outer_ref[...].astype(F32)
        for side, at, row, slots in ((0, 7, -1, (0, 1, 2)), (1, 8 + PIX, 1, (5, 6, 7))):
            both = jnp.where(even, outer, inner) if side == 0 else jnp.where(even, inner, outer)

            def picked(slot):
                return jnp.where(local(slot, row) == 0, both[0:1], both[1:2]) * known(slot)

            rows_f[0, at : at + 1, :] = picked(slots[0])[:, (GROUPS - 1) * LANES :]
            middle = picked(slots[1])
            for k in range(GROUPS):
                rows_f[k + 1, at : at + 1, :] = middle[:, k * LANES : (k + 1) * LANES]
            rows_f[GROUPS + 1, at : at + 1, :] = picked(slots[2])[:, :LANES]
        for k in range(GROUPS + 2):
            for n, first in enumerate((7, 8, 9, 10)):
                xs[n, k] = rows_f[k, pl.ds(first, HALF, stride=2), :].astype(BF16)

    for m in range(QUADS):
        group = 2 * (step * QUADS + m)
        for odd in range(2):
            at = (odd * QUADS + m) * HALF
            for r in range(3):
                for k in range(4):
                    lhs[at : at + HALF, r * 512 + k * LANES : r * 512 + (k + 1) * LANES] = xs[odd + r, group + k]
    target = jnp.concatenate(
        [cot_ref[:, (2 * m + h) * CH_OUT : (2 * m + h + 1) * CH_OUT] for h in range(2) for m in range(QUADS)], axis=0
    ).astype(F32)
    loss, gnext, gms, gconv = chain(lhs[...], target, wc[...], wms[...], wn_ref[...])
    acc_loss[...] += loss
    acc_next[...] += gnext
    acc_ms[...] += gms
    acc_conv[...] += gconv

    for number, first, second in ((0, keep_ref, send_ref), (1, send_ref, keep_ref)):
        @pl.when((step == STEPS - 1) & (core == number))
        def _(first=first, second=second):
            pack(ids_ref, acc_loss[...], acc_next[...], acc_ms[...], acc_conv, first, second)


def in_vmem(array):
    return pltpu.with_memory_space_constraint(array, pltpu.VMEM)


def run_tile(ids, adjacency, images, inner, outer, cotangent, conv_weight, mix_weight, skip_weight, next_weight):
    def pair_of(slot):
        def index(step, ids_ref, adj_ref):
            near = adj_ref[ids_ref[0], slot] - ids_ref[1] * 2
            return (0, jnp.clip(near, 0, 1), 0, GROUPS - 1 if slot == 3 else 0)

        return index

    def whole(shape):
        return pl.BlockSpec(shape, lambda step, ids_ref, adj_ref: (0,) * len(shape))

    return pl.pallas_call(
        tile_kernel,
        out_shape=[pltpu.VMEM((ROWS, LANES), BF16)] * 2,
        grid_spec=pltpu.PrefetchScalarGridSpec(
            num_scalar_prefetch=2,
            grid=(STEPS,),
            in_specs=[
                pl.BlockSpec((None, None, PIX, PIX * CH_IN), lambda step, ids_ref, adj_ref: (0, ids_ref[0], 0, 0)),
                pl.BlockSpec((None, None, PIX, LANES), pair_of(3)),
                pl.BlockSpec((None, None, PIX, LANES), pair_of(4)),
                pl.BlockSpec(memory_space=pltpu.VMEM),
                pl.BlockSpec(memory_space=pltpu.VMEM),
                pl.BlockSpec((None, None, HALF, 2 * QUADS * CH_OUT), lambda step, ids_ref, adj_ref: (0, ids_ref[0], 0, step)),
                whole((CH_IN, 9 * CH_IN)),
                whole((CH_IN, CH_MID)),
                whole((CH_IN, CH_MID)),
                whole((CH_MID, CH_OUT)),
            ],
            out_specs=[pl.BlockSpec(memory_space=pltpu.VMEM)] * 2,
            scratch_shapes=[
                pltpu.VMEM((GROUPS + 2, 80, LANES), F32),
                pltpu.VMEM((4, GROUPS + 2, HALF, LANES), BF16),
                pltpu.VMEM((2 * QUADS * HALF, 1536), BF16),
                pltpu.VMEM((1536, 256), BF16),
                pltpu.VMEM((256, 512), BF16),
                pltpu.VMEM((1, CH_OUT), F32),
                pltpu.VMEM((CH_MID, CH_OUT), F32),
                pltpu.VMEM((256, 512), F32),
                pltpu.VMEM((256, 1536), F32),
            ],
        ),
        name="tile",
    )(ids, adjacency, images, images, images, inner, outer, cotangent, conv_weight, mix_weight, skip_weight, next_weight)


def unpack_kernel(ids_ref, own_ref, other_ref, conv_ref, mix_ref, skip_ref, next_ref, loss_ref):
    def unpack(wide_ref, rest_ref):
        for k in range(4):
            next_ref[:, k * LANES : (k + 1) * LANES] = wide_ref[k * 256 : (k + 1) * 256, :].astype(F32)
        for k in range(9):
            tap = rest_ref[k * 64 : (k + 1) * 64, :].astype(F32)
            conv_ref[:, k * CH_IN : (k + 1) * CH_IN] = tap[:, :CH_IN]
        for k, ref in enumerate((mix_ref, skip_ref)):
            for n in range(2):
                at = 576 + k * 128 + n * 64
                ref[:, n * LANES : (n + 1) * LANES] = rest_ref[at : at + 64, :].astype(F32)
        loss = rest_ref[832:840, :].astype(F32) + rest_ref[840:848, :].astype(F32)
        count = loss_ref.shape[1]
        for k in range(loss_ref.shape[0]):
            loss_ref[k : k + 1, :] = loss[0:1, k * count : (k + 1) * count]

    @pl.when(ids_ref[0] == 0)
    def _():
        unpack(own_ref, other_ref)

    @pl.when(ids_ref[0] != 0)
    def _():
        unpack(other_ref, own_ref)


def run_unpack(ids, own, other, slides, tiles):
    return pl.pallas_call(
        unpack_kernel,
        out_shape=[
            jax.ShapeDtypeStruct((CH_IN, 9 * CH_IN), F32),
            jax.ShapeDtypeStruct((CH_IN, CH_MID), F32),
            jax.ShapeDtypeStruct((CH_IN, CH_MID), F32),
            jax.ShapeDtypeStruct((CH_MID, CH_OUT), F32),
            jax.ShapeDtypeStruct((slides, tiles), F32),
        ],
        in_specs=[pl.BlockSpec(memory_space=pltpu.SMEM), pl.BlockSpec(memory_space=pltpu.VMEM), pl.BlockSpec(memory_space=pltpu.VMEM)],
        out_specs=[pl.BlockSpec(memory_space=pltpu.VMEM)] * 5,
        name="unpack",
    )(ids, own, other)


def body(slides, rows, images, adjacency, conv_weight, mix_weight, skip_weight, next_weight, cotangent):
    core = lax.axis_index("segment").astype(jnp.int32)
    row = lax.axis_index("tile").astype(jnp.int32)
    place = lax.axis_index("slide").astype(jnp.int32) * (2 * rows) + row * 2 + core
    ids = jnp.stack([core, row, place])
    top, low = images[0, :, 0], images[0, :, PIX - 1]
    even = row % 2 == 0
    swaps = [[(i, i + 1) for i in range(first, rows - 1, 2)] for first in (0, 1)]
    swaps = [pairs + [(j, i) for i, j in pairs] for pairs in swaps]
    inner = lax.ppermute(jnp.where(even, low, top), "tile", swaps[0])
    outer = lax.ppermute(jnp.where(even, top, low), "tile", swaps[1])
    keep, send = run_tile(
        ids, adjacency[0], images, in_vmem(inner), in_vmem(outer), cotangent, conv_weight.T, mix_weight, skip_weight, next_weight
    )
    swap = [(0, 1), (1, 0)]
    group = ("slide", "tile")
    parts = slides * rows
    got = lax.ppermute(send, "segment", swap)
    own = (keep.astype(F32) + got.astype(F32)).astype(BF16).reshape(parts, ROWS // parts, LANES)
    pieces = lax.all_to_all(own, group, 0, 0, tiled=True)
    total = jnp.sum(pieces.astype(F32), axis=0).astype(BF16)
    copies = jnp.broadcast_to(total[None], (parts, ROWS // parts, LANES))
    own = lax.all_to_all(copies, group, 0, 0, tiled=True).reshape(ROWS, LANES)
    other = lax.ppermute(own, "segment", swap)
    conv, mix, skip, nxt, loss = run_unpack(ids, in_vmem(own), in_vmem(other), slides, 2 * rows)
    return conv.T, mix, skip, nxt, loss


def solution(mesh):
    placed = (
        P("slide", "tile", None, None),
        P("slide", "tile", None),
        P(),
        P(),
        P(),
        P(),
        P("slide", "tile", None, None),
    )
    return jax.shard_map(
        functools.partial(body, mesh.shape["slide"], mesh.shape["tile"]),
        mesh=mesh,
        in_specs=placed,
        out_specs=(P(), P(), P(), P(), P()),
        check_vma=False,
    )
```

```python
import functools

import jax
import jax.numpy as jnp
from jax import lax
from jax.experimental import pallas as pl
from jax.experimental.pallas import tpu as pltpu
from jax.sharding import PartitionSpec as P

CH_IN = 64
CH_MID = 256
CH_OUT = 512
PIX = 64
HALF = 32
LANES = 128
GROUPS = PIX * CH_IN // LANES
QUADS = 16
ROWS = 1024
F32 = jnp.float32
BF16 = jnp.bfloat16


def dot_nn(a, b):
    return jnp.dot(a, b, preferred_element_type=F32)


def dot_tn(a, b):
    return lax.dot_general(a, b, (((0,), (0,)), ((), ())), preferred_element_type=F32)


def dot_nt(a, b):
    return lax.dot_general(a, b, (((1,), (1,)), ((), ())), preferred_element_type=F32)


def silu_and_slope(v):
    sig = 0.5 * jnp.tanh(0.5 * v) + 0.5
    out = v * sig
    return out, sig + out * (1.0 - sig)


def chain(lhs, target, wc, wms, wn):
    half = lhs.shape[0] // 2
    hid, slope_pre = silu_and_slope(dot_nn(lhs, wc))
    hid = hid.astype(BF16)
    pairs, slopes, pooled = [], [], []
    for h in range(2):
        x = lhs[:, 5 * LANES + h * LANES : 6 * LANES + h * LANES]
        hx = jnp.concatenate([hid[:, h * LANES : (h + 1) * LANES], x], axis=1)
        act, slope = silu_and_slope(dot_nn(hx, wms))
        act = act.astype(BF16).astype(F32)
        side = act[:, :CH_MID] + act[:, CH_MID:]
        pooled.append((0.25 * (side[:half] + side[half:])).astype(BF16))
        pairs.append(hx)
        slopes.append(slope)
    pooled = jnp.concatenate(pooled, axis=0)
    out, slope_out = silu_and_slope(dot_nn(pooled, wn))
    loss = jnp.sum(out * target, axis=0, keepdims=True)
    grad_out = (target * slope_out).astype(BF16)
    grad_next = dot_tn(pooled, grad_out)
    grad_pooled = dot_nt(grad_out, wn).astype(BF16).astype(F32) * 0.25
    grad_ms, back = None, []
    for h in range(2):
        g = grad_pooled[h * half : (h + 1) * half]
        g = jnp.concatenate([g, g], axis=0)
        g = jnp.concatenate([g, g], axis=1)
        grad_sum = (g * slopes[h]).astype(BF16)
        part = dot_tn(pairs[h], grad_sum)
        grad_ms = part if grad_ms is None else grad_ms + part
        back.append(dot_nt(grad_sum, wms[:LANES]))
    grad_pre = (jnp.concatenate(back, axis=1) * slope_pre).astype(BF16)
    return loss, grad_next, grad_ms, dot_tn(grad_pre, lhs)


def build_weights(conv_ref, mix_ref, skip_ref, wc, wms):
    zero = jnp.zeros((CH_IN, CH_IN), BF16)
    taps = []
    for k in range(9):
        if k % 2 == 0:
            wide = min(LANES, (9 - k) * CH_IN)
            pair = conv_ref[:, k * CH_IN : k * CH_IN + wide].astype(F32).T.astype(BF16)
        taps.append(pair[(k % 2) * CH_IN : (k % 2 + 1) * CH_IN, :])
    for r in range(3):
        for w in range(8):
            row = []
            for b in range(4):
                c = w - b - 1
                row.append(taps[3 * r + c] if 0 <= c <= 2 else zero)
            wc[r * 512 + w * CH_IN : r * 512 + (w + 1) * CH_IN, :] = jnp.concatenate(row, axis=1)
    wms[...] = jnp.zeros_like(wms)
    for k in range(2):
        wms[k * CH_IN : (k + 1) * CH_IN, k * CH_MID : (k + 1) * CH_MID] = mix_ref[...]
        wms[(2 + k) * CH_IN : (3 + k) * CH_IN, k * CH_MID : (k + 1) * CH_MID] = skip_ref[...]


def sums_of_taps(acc):
    taps = []
    for r in range(3):
        for c in range(3):
            parts = [None, None]
            for b in range(4):
                w = b + c + 1
                at = r * 512 + (w // 2) * LANES
                piece = acc[b * CH_IN : (b + 1) * CH_IN, at : at + LANES]
                parts[w % 2] = piece if parts[w % 2] is None else parts[w % 2] + piece
            taps.append(parts[0] + pltpu.roll(parts[1], CH_IN, 1))
    return taps


def pack(ids_ref, loss, gnext, gms, gconv, next_ref, rest_ref):
    for k in range(4):
        next_ref[k * 256 : (k + 1) * 256, :] = gnext[:, k * LANES : (k + 1) * LANES].astype(BF16)
    for k, tap in enumerate(sums_of_taps(gconv)):
        rest_ref[k * 64 : (k + 1) * 64, :] = tap.astype(BF16)
    for k in range(2):
        low, high = gms[2 * k * CH_IN : (2 * k + 1) * CH_IN, :CH_MID], gms[(2 * k + 1) * CH_IN : (2 * k + 2) * CH_IN, CH_MID:]
        both = (low + high).astype(BF16)
        for n in range(2):
            at = 576 + k * 128 + n * 64
            rest_ref[at : at + 64, :] = both[:, n * LANES : (n + 1) * LANES]
    total = jnp.sum(loss)
    lane = lax.broadcasted_iota(jnp.int32, (8, LANES), 1)
    value = jnp.where(lane == ids_ref[2], total, 0.0)
    upper = value.astype(BF16)
    rest_ref[832:840, :] = upper
    rest_ref[840:848, :] = (value - upper.astype(F32)).astype(BF16)
    rest_ref[848:ROWS, :] = jnp.zeros((ROWS - 848, LANES), BF16)


def tile_kernel(ids_ref, adj_ref, img_ref, west_ref, east_ref, inner_ref, outer_ref, cot_ref, conv_ref, mix_ref, skip_ref, wn_ref,
                keep_ref, send_ref, rows_f, xs, lhs, wc, wms, acc_conv):
    core = ids_ref[0]

    def known(slot):
        return (adj_ref[core, slot] >= 0).astype(F32)

    def local(slot, row):
        return jnp.clip(adj_ref[core, slot] - (ids_ref[1] + row) * 2, 0, 1)

    build_weights(conv_ref, mix_ref, skip_ref, wc, wms)
    for k in range(GROUPS):
        rows_f[k + 1, 8 : 8 + PIX, :] = img_ref[:, k * LANES : (k + 1) * LANES].astype(F32)
    rows_f[0, 8 : 8 + PIX, :] = west_ref[...].astype(F32) * known(3)
    rows_f[GROUPS + 1, 8 : 8 + PIX, :] = east_ref[...].astype(F32) * known(4)
    even = ids_ref[1] % 2 == 0
    inner, outer = inner_ref[...].astype(F32), outer_ref[...].astype(F32)
    for side, at, row, slots in ((0, 7, -1, (0, 1, 2)), (1, 8 + PIX, 1, (5, 6, 7))):
        both = jnp.where(even, outer, inner) if side == 0 else jnp.where(even, inner, outer)

        def picked(slot):
            return jnp.where(local(slot, row) == 0, both[0:1], both[1:2]) * known(slot)

        rows_f[0, at : at + 1, :] = picked(slots[0])[:, (GROUPS - 1) * LANES :]
        middle = picked(slots[1])
        for k in range(GROUPS):
            rows_f[k + 1, at : at + 1, :] = middle[:, k * LANES : (k + 1) * LANES]
        rows_f[GROUPS + 1, at : at + 1, :] = picked(slots[2])[:, :LANES]
    for k in range(GROUPS + 2):
        for n, first in enumerate((7, 8, 9, 10)):
            xs[n, k] = rows_f[k, pl.ds(first, HALF, stride=2), :].astype(BF16)

    for m in range(QUADS):
        group = 2 * m
        for odd in range(2):
            at = (odd * QUADS + m) * HALF
            for r in range(3):
                for k in range(4):
                    lhs[at : at + HALF, r * 512 + k * LANES : r * 512 + (k + 1) * LANES] = xs[odd + r, group + k]
    target = jnp.concatenate(
        [cot_ref[:, (2 * m + h) * CH_OUT : (2 * m + h + 1) * CH_OUT] for h in range(2) for m in range(QUADS)], axis=0
    ).astype(F32)
    loss, gnext, gms, gconv = chain(lhs[...], target, wc[...], wms[...], wn_ref[...])
    acc_conv[...] = gconv

    for number, first, second in ((0, keep_ref, send_ref), (1, send_ref, keep_ref)):
        @pl.when(core == number)
        def _(first=first, second=second):
            pack(ids_ref, loss, gnext, gms, acc_conv, first, second)


def in_vmem(array):
    return pltpu.with_memory_space_constraint(array, pltpu.VMEM)


def run_tile(ids, adjacency, images, inner, outer, cotangent, conv_weight, mix_weight, skip_weight, next_weight):
    def pair_of(slot):
        def index(step, ids_ref, adj_ref):
            near = adj_ref[ids_ref[0], slot] - ids_ref[1] * 2
            return (0, jnp.clip(near, 0, 1), 0, GROUPS - 1 if slot == 3 else 0)

        return index

    def whole(shape):
        return pl.BlockSpec(shape, lambda step, ids_ref, adj_ref: (0,) * len(shape))

    return pl.pallas_call(
        tile_kernel,
        out_shape=[pltpu.VMEM((ROWS, LANES), BF16)] * 2,
        grid_spec=pltpu.PrefetchScalarGridSpec(
            num_scalar_prefetch=2,
            grid=(1,),
            in_specs=[
                pl.BlockSpec((None, None, PIX, PIX * CH_IN), lambda step, ids_ref, adj_ref: (0, ids_ref[0], 0, 0)),
                pl.BlockSpec((None, None, PIX, LANES), pair_of(3)),
                pl.BlockSpec((None, None, PIX, LANES), pair_of(4)),
                pl.BlockSpec(memory_space=pltpu.VMEM),
                pl.BlockSpec(memory_space=pltpu.VMEM),
                pl.BlockSpec((None, None, HALF, HALF * CH_OUT), lambda step, ids_ref, adj_ref: (0, ids_ref[0], 0, 0)),
                whole((CH_IN, 9 * CH_IN)),
                whole((CH_IN, CH_MID)),
                whole((CH_IN, CH_MID)),
                whole((CH_MID, CH_OUT)),
            ],
            out_specs=[pl.BlockSpec(memory_space=pltpu.VMEM)] * 2,
            scratch_shapes=[
                pltpu.VMEM((GROUPS + 2, 80, LANES), F32),
                pltpu.VMEM((4, GROUPS + 2, HALF, LANES), BF16),
                pltpu.VMEM((2 * QUADS * HALF, 1536), BF16),
                pltpu.VMEM((1536, 256), BF16),
                pltpu.VMEM((256, 512), BF16),
                pltpu.VMEM((256, 1536), F32),
            ],
        ),
        name="tile",
    )(ids, adjacency, images, images, images, inner, outer, cotangent, conv_weight, mix_weight, skip_weight, next_weight)


def unpack_kernel(ids_ref, own_ref, other_ref, conv_ref, mix_ref, skip_ref, next_ref, loss_ref):
    def unpack(wide_ref, rest_ref):
        for k in range(4):
            next_ref[:, k * LANES : (k + 1) * LANES] = wide_ref[k * 256 : (k + 1) * 256, :].astype(F32)
        for k in range(9):
            tap = rest_ref[k * 64 : (k + 1) * 64, :].astype(F32)
            conv_ref[:, k * CH_IN : (k + 1) * CH_IN] = tap[:, :CH_IN]
        for k, ref in enumerate((mix_ref, skip_ref)):
            for n in range(2):
                at = 576 + k * 128 + n * 64
                ref[:, n * LANES : (n + 1) * LANES] = rest_ref[at : at + 64, :].astype(F32)
        loss = rest_ref[832:840, :].astype(F32) + rest_ref[840:848, :].astype(F32)
        count = loss_ref.shape[1]
        for k in range(loss_ref.shape[0]):
            loss_ref[k : k + 1, :] = loss[0:1, k * count : (k + 1) * count]

    @pl.when(ids_ref[0] == 0)
    def _():
        unpack(own_ref, other_ref)

    @pl.when(ids_ref[0] != 0)
    def _():
        unpack(other_ref, own_ref)


def run_unpack(ids, own, other, slides, tiles):
    return pl.pallas_call(
        unpack_kernel,
        out_shape=[
            jax.ShapeDtypeStruct((CH_IN, 9 * CH_IN), F32),
            jax.ShapeDtypeStruct((CH_IN, CH_MID), F32),
            jax.ShapeDtypeStruct((CH_IN, CH_MID), F32),
            jax.ShapeDtypeStruct((CH_MID, CH_OUT), F32),
            jax.ShapeDtypeStruct((slides, tiles), F32),
        ],
        in_specs=[pl.BlockSpec(memory_space=pltpu.SMEM), pl.BlockSpec(memory_space=pltpu.VMEM), pl.BlockSpec(memory_space=pltpu.VMEM)],
        out_specs=[pl.BlockSpec(memory_space=pltpu.VMEM)] * 5,
        name="unpack",
    )(ids, own, other)


def body(slides, rows, images, adjacency, conv_weight, mix_weight, skip_weight, next_weight, cotangent):
    core = lax.axis_index("segment").astype(jnp.int32)
    row = lax.axis_index("tile").astype(jnp.int32)
    place = lax.axis_index("slide").astype(jnp.int32) * (2 * rows) + row * 2 + core
    ids = jnp.stack([core, row, place])
    top, low = images[0, :, 0], images[0, :, PIX - 1]
    even = row % 2 == 0
    swaps = [[(i, i + 1) for i in range(first, rows - 1, 2)] for first in (0, 1)]
    swaps = [pairs + [(j, i) for i, j in pairs] for pairs in swaps]
    inner = lax.ppermute(jnp.where(even, low, top), "tile", swaps[0])
    outer = lax.ppermute(jnp.where(even, top, low), "tile", swaps[1])
    keep, send = run_tile(
        ids, adjacency[0], images, in_vmem(inner), in_vmem(outer), cotangent, conv_weight.T, mix_weight, skip_weight, next_weight
    )
    swap = [(0, 1), (1, 0)]
    group = ("slide", "tile")
    parts = slides * rows
    got = lax.ppermute(send, "segment", swap)
    own = (keep.astype(F32) + got.astype(F32)).astype(BF16).reshape(parts, ROWS // parts, LANES)
    pieces = lax.all_to_all(own, group, 0, 0, tiled=True)
    total = jnp.sum(pieces.astype(F32), axis=0).astype(BF16)
    copies = jnp.broadcast_to(total[None], (parts, ROWS // parts, LANES))
    own = lax.all_to_all(copies, group, 0, 0, tiled=True).reshape(ROWS, LANES)
    other = lax.ppermute(own, "segment", swap)
    conv, mix, skip, nxt, loss = run_unpack(ids, in_vmem(own), in_vmem(other), slides, 2 * rows)
    return conv.T, mix, skip, nxt, loss


def solution(mesh):
    placed = (
        P("slide", "tile", None, None),
        P("slide", "tile", None),
        P(),
        P(),
        P(),
        P(),
        P("slide", "tile", None, None),
    )
    return jax.shard_map(
        functools.partial(body, mesh.shape["slide"], mesh.shape["tile"]),
        mesh=mesh,
        in_specs=placed,
        out_specs=(P(), P(), P(), P(), P()),
        check_vma=False,
    )
```

```python
import functools

import jax
import jax.numpy as jnp
from jax import lax
from jax.experimental import pallas as pl
from jax.experimental.pallas import tpu as pltpu
from jax.sharding import PartitionSpec as P

CH_IN = 64
CH_MID = 256
CH_OUT = 512
PIX = 64
HALF = 32
LANES = 128
GROUPS = PIX * CH_IN // LANES
QUADS = 16
ROWS = 1024
F32 = jnp.float32
BF16 = jnp.bfloat16


def dot_nn(a, b):
    return jnp.dot(a, b, preferred_element_type=F32)


def dot_tn(a, b):
    return lax.dot_general(a, b, (((0,), (0,)), ((), ())), preferred_element_type=F32)


def dot_nt(a, b):
    return lax.dot_general(a, b, (((1,), (1,)), ((), ())), preferred_element_type=F32)


def silu_and_slope(v):
    sig = 0.5 * jnp.tanh(0.5 * v) + 0.5
    out = v * sig
    return out, sig + out * (1.0 - sig)


def chain(lhs, target, wc, wms, wn):
    half = lhs.shape[0] // 2
    hid, slope_pre = silu_and_slope(dot_nn(lhs, wc))
    hid = hid.astype(BF16)
    pairs, slopes, pooled = [], [], []
    for h in range(2):
        x = lhs[:, 5 * LANES + h * LANES : 6 * LANES + h * LANES]
        hx = jnp.concatenate([hid[:, h * LANES : (h + 1) * LANES], x], axis=1)
        act, slope = silu_and_slope(dot_nn(hx, wms).astype(BF16))
        act = act.astype(F32)
        side = act[:, :CH_MID] + act[:, CH_MID:]
        pooled.append((0.25 * (side[:half] + side[half:])).astype(BF16))
        pairs.append(hx)
        slopes.append(slope)
    pooled = jnp.concatenate(pooled, axis=0)
    out, slope_out = silu_and_slope(dot_nn(pooled, wn))
    loss = jnp.sum(out * target, axis=0, keepdims=True)
    grad_out = (target * slope_out).astype(BF16)
    grad_next = dot_tn(pooled, grad_out)
    grad_pooled = dot_nt(grad_out, wn).astype(BF16) * 0.25
    grad_ms, back = None, []
    for h in range(2):
        g = grad_pooled[h * half : (h + 1) * half]
        g = jnp.concatenate([g, g], axis=0)
        g = jnp.concatenate([g, g], axis=1)
        grad_sum = g * slopes[h]
        part = dot_tn(pairs[h], grad_sum)
        grad_ms = part if grad_ms is None else grad_ms + part
        back.append(dot_nt(grad_sum, wms[:LANES]))
    grad_pre = (jnp.concatenate(back, axis=1) * slope_pre).astype(BF16)
    return loss, grad_next, grad_ms, dot_tn(grad_pre, lhs)


def build_weights(conv_ref, mix_ref, skip_ref, wc, wms):
    zero = jnp.zeros((CH_IN, CH_IN), BF16)
    taps = []
    for k in range(9):
        if k % 2 == 0:
            wide = min(LANES, (9 - k) * CH_IN)
            pair = conv_ref[:, k * CH_IN : k * CH_IN + wide].astype(F32).T.astype(BF16)
        taps.append(pair[(k % 2) * CH_IN : (k % 2 + 1) * CH_IN, :])
    for r in range(3):
        for w in range(8):
            row = []
            for b in range(4):
                c = w - b - 1
                row.append(taps[3 * r + c] if 0 <= c <= 2 else zero)
            wc[r * 512 + w * CH_IN : r * 512 + (w + 1) * CH_IN, :] = jnp.concatenate(row, axis=1)
    wms[...] = jnp.zeros_like(wms)
    for k in range(2):
        wms[k * CH_IN : (k + 1) * CH_IN, k * CH_MID : (k + 1) * CH_MID] = mix_ref[...]
        wms[(2 + k) * CH_IN : (3 + k) * CH_IN, k * CH_MID : (k + 1) * CH_MID] = skip_ref[...]


def sums_of_taps(acc):
    taps = []
    for r in range(3):
        for c in range(3):
            parts = [None, None]
            for b in range(4):
                w = b + c + 1
                at = r * 512 + (w // 2) * LANES
                piece = acc[b * CH_IN : (b + 1) * CH_IN, at : at + LANES]
                parts[w % 2] = piece if parts[w % 2] is None else parts[w % 2] + piece
            taps.append(parts[0] + pltpu.roll(parts[1], CH_IN, 1))
    return taps


def pack(ids_ref, loss, gnext, gms, gconv, next_ref, rest_ref):
    for k in range(4):
        next_ref[k * 256 : (k + 1) * 256, :] = gnext[:, k * LANES : (k + 1) * LANES].astype(BF16)
    for k, tap in enumerate(sums_of_taps(gconv)):
        rest_ref[k * 64 : (k + 1) * 64, :] = tap.astype(BF16)
    for k in range(2):
        low, high = gms[2 * k * CH_IN : (2 * k + 1) * CH_IN, :CH_MID], gms[(2 * k + 1) * CH_IN : (2 * k + 2) * CH_IN, CH_MID:]
        both = (low + high).astype(BF16)
        for n in range(2):
            at = 576 + k * 128 + n * 64
            rest_ref[at : at + 64, :] = both[:, n * LANES : (n + 1) * LANES]
    total = jnp.sum(loss)
    lane = lax.broadcasted_iota(jnp.int32, (8, LANES), 1)
    value = jnp.where(lane == ids_ref[2], total, 0.0)
    upper = value.astype(BF16)
    rest_ref[832:840, :] = upper
    rest_ref[840:848, :] = (value - upper.astype(F32)).astype(BF16)
    rest_ref[848:ROWS, :] = jnp.zeros((ROWS - 848, LANES), BF16)


def tile_kernel(ids_ref, adj_ref, img_ref, west_ref, east_ref, inner_ref, outer_ref, cot_ref, conv_ref, mix_ref, skip_ref, wn_ref,
                keep_ref, send_ref, rows_f, xs, lhs, wc, wms, acc_conv):
    core = ids_ref[0]

    def known(slot):
        return (adj_ref[core, slot] >= 0).astype(F32)

    def local(slot, row):
        return jnp.clip(adj_ref[core, slot] - (ids_ref[1] + row) * 2, 0, 1)

    build_weights(conv_ref, mix_ref, skip_ref, wc, wms)
    for k in range(GROUPS):
        rows_f[k + 1, 8 : 8 + PIX, :] = img_ref[:, k * LANES : (k + 1) * LANES].astype(F32)
    rows_f[0, 8 : 8 + PIX, :] = west_ref[...].astype(F32) * known(3)
    rows_f[GROUPS + 1, 8 : 8 + PIX, :] = east_ref[...].astype(F32) * known(4)
    even = ids_ref[1] % 2 == 0
    inner, outer = inner_ref[...].astype(F32), outer_ref[...].astype(F32)
    for side, at, row, slots in ((0, 7, -1, (0, 1, 2)), (1, 8 + PIX, 1, (5, 6, 7))):
        both = jnp.where(even, outer, inner) if side == 0 else jnp.where(even, inner, outer)

        def picked(slot):
            return jnp.where(local(slot, row) == 0, both[0:1], both[1:2]) * known(slot)

        rows_f[0, at : at + 1, :] = picked(slots[0])[:, (GROUPS - 1) * LANES :]
        middle = picked(slots[1])
        for k in range(GROUPS):
            rows_f[k + 1, at : at + 1, :] = middle[:, k * LANES : (k + 1) * LANES]
        rows_f[GROUPS + 1, at : at + 1, :] = picked(slots[2])[:, :LANES]
    for k in range(GROUPS + 2):
        for n, first in enumerate((7, 8, 9, 10)):
            xs[n, k] = rows_f[k, pl.ds(first, HALF, stride=2), :].astype(BF16)

    for m in range(QUADS):
        group = 2 * m
        for odd in range(2):
            at = (odd * QUADS + m) * HALF
            for r in range(3):
                for k in range(4):
                    lhs[at : at + HALF, r * 512 + k * LANES : r * 512 + (k + 1) * LANES] = xs[odd + r, group + k]
    target = jnp.concatenate(
        [cot_ref[:, (2 * m + h) * CH_OUT : (2 * m + h + 1) * CH_OUT] for h in range(2) for m in range(QUADS)], axis=0
    ).astype(F32)
    loss, gnext, gms, gconv = chain(lhs[...], target, wc[...], wms[...], wn_ref[...])
    acc_conv[...] = gconv

    for number, first, second in ((0, keep_ref, send_ref), (1, send_ref, keep_ref)):
        @pl.when(core == number)
        def _(first=first, second=second):
            pack(ids_ref, loss, gnext, gms, acc_conv, first, second)


def in_vmem(array):
    return pltpu.with_memory_space_constraint(array, pltpu.VMEM)


def run_tile(ids, adjacency, images, inner, outer, cotangent, conv_weight, mix_weight, skip_weight, next_weight):
    def pair_of(slot):
        def index(step, ids_ref, adj_ref):
            near = adj_ref[ids_ref[0], slot] - ids_ref[1] * 2
            return (0, jnp.clip(near, 0, 1), 0, GROUPS - 1 if slot == 3 else 0)

        return index

    def whole(shape):
        return pl.BlockSpec(shape, lambda step, ids_ref, adj_ref: (0,) * len(shape))

    return pl.pallas_call(
        tile_kernel,
        out_shape=[pltpu.VMEM((ROWS, LANES), BF16)] * 2,
        grid_spec=pltpu.PrefetchScalarGridSpec(
            num_scalar_prefetch=2,
            grid=(1,),
            in_specs=[
                pl.BlockSpec((None, None, PIX, PIX * CH_IN), lambda step, ids_ref, adj_ref: (0, ids_ref[0], 0, 0)),
                pl.BlockSpec((None, None, PIX, LANES), pair_of(3)),
                pl.BlockSpec((None, None, PIX, LANES), pair_of(4)),
                pl.BlockSpec(memory_space=pltpu.VMEM),
                pl.BlockSpec(memory_space=pltpu.VMEM),
                pl.BlockSpec((None, None, HALF, HALF * CH_OUT), lambda step, ids_ref, adj_ref: (0, ids_ref[0], 0, 0)),
                whole((CH_IN, 9 * CH_IN)),
                whole((CH_IN, CH_MID)),
                whole((CH_IN, CH_MID)),
                whole((CH_MID, CH_OUT)),
            ],
            out_specs=[pl.BlockSpec(memory_space=pltpu.VMEM)] * 2,
            scratch_shapes=[
                pltpu.VMEM((GROUPS + 2, 80, LANES), F32),
                pltpu.VMEM((4, GROUPS + 2, HALF, LANES), BF16),
                pltpu.VMEM((2 * QUADS * HALF, 1536), BF16),
                pltpu.VMEM((1536, 256), BF16),
                pltpu.VMEM((256, 512), BF16),
                pltpu.VMEM((256, 1536), F32),
            ],
        ),
        name="tile",
    )(ids, adjacency, images, images, images, inner, outer, cotangent, conv_weight, mix_weight, skip_weight, next_weight)


def unpack_kernel(ids_ref, own_ref, other_ref, conv_ref, mix_ref, skip_ref, next_ref, loss_ref):
    def unpack(wide_ref, rest_ref):
        for k in range(4):
            next_ref[:, k * LANES : (k + 1) * LANES] = wide_ref[k * 256 : (k + 1) * 256, :].astype(F32)
        for k in range(9):
            tap = rest_ref[k * 64 : (k + 1) * 64, :].astype(F32)
            conv_ref[:, k * CH_IN : (k + 1) * CH_IN] = tap[:, :CH_IN]
        for k, ref in enumerate((mix_ref, skip_ref)):
            for n in range(2):
                at = 576 + k * 128 + n * 64
                ref[:, n * LANES : (n + 1) * LANES] = rest_ref[at : at + 64, :].astype(F32)
        loss = rest_ref[832:840, :].astype(F32) + rest_ref[840:848, :].astype(F32)
        count = loss_ref.shape[1]
        for k in range(loss_ref.shape[0]):
            loss_ref[k : k + 1, :] = loss[0:1, k * count : (k + 1) * count]

    @pl.when(ids_ref[0] == 0)
    def _():
        unpack(own_ref, other_ref)

    @pl.when(ids_ref[0] != 0)
    def _():
        unpack(other_ref, own_ref)


def run_unpack(ids, own, other, slides, tiles):
    return pl.pallas_call(
        unpack_kernel,
        out_shape=[
            jax.ShapeDtypeStruct((CH_IN, 9 * CH_IN), F32),
            jax.ShapeDtypeStruct((CH_IN, CH_MID), F32),
            jax.ShapeDtypeStruct((CH_IN, CH_MID), F32),
            jax.ShapeDtypeStruct((CH_MID, CH_OUT), F32),
            jax.ShapeDtypeStruct((slides, tiles), F32),
        ],
        in_specs=[pl.BlockSpec(memory_space=pltpu.SMEM), pl.BlockSpec(memory_space=pltpu.VMEM), pl.BlockSpec(memory_space=pltpu.VMEM)],
        out_specs=[pl.BlockSpec(memory_space=pltpu.VMEM)] * 5,
        name="unpack",
    )(ids, own, other)


def body(slides, rows, images, adjacency, conv_weight, mix_weight, skip_weight, next_weight, cotangent):
    core = lax.axis_index("segment").astype(jnp.int32)
    row = lax.axis_index("tile").astype(jnp.int32)
    place = lax.axis_index("slide").astype(jnp.int32) * (2 * rows) + row * 2 + core
    ids = jnp.stack([core, row, place])
    top, low = images[0, :, 0], images[0, :, PIX - 1]
    even = row % 2 == 0
    swaps = [[(i, i + 1) for i in range(first, rows - 1, 2)] for first in (0, 1)]
    swaps = [pairs + [(j, i) for i, j in pairs] for pairs in swaps]
    inner = lax.ppermute(jnp.where(even, low, top), "tile", swaps[0])
    outer = lax.ppermute(jnp.where(even, top, low), "tile", swaps[1])
    keep, send = run_tile(
        ids, adjacency[0], images, in_vmem(inner), in_vmem(outer), cotangent, conv_weight.T, mix_weight, skip_weight, next_weight
    )
    swap = [(0, 1), (1, 0)]
    group = ("slide", "tile")
    parts = slides * rows
    got = lax.ppermute(send, "segment", swap)
    own = (keep.astype(F32) + got.astype(F32)).astype(BF16).reshape(parts, ROWS // parts, LANES)
    pieces = lax.all_to_all(own, group, 0, 0, tiled=True)
    total = jnp.sum(pieces.astype(F32), axis=0).astype(BF16)
    copies = jnp.broadcast_to(total[None], (parts, ROWS // parts, LANES))
    own = lax.all_to_all(copies, group, 0, 0, tiled=True).reshape(ROWS, LANES)
    other = lax.ppermute(own, "segment", swap)
    conv, mix, skip, nxt, loss = run_unpack(ids, in_vmem(own), in_vmem(other), slides, 2 * rows)
    return conv.T, mix, skip, nxt, loss


def solution(mesh):
    placed = (
        P("slide", "tile", None, None),
        P("slide", "tile", None),
        P(),
        P(),
        P(),
        P(),
        P("slide", "tile", None, None),
    )
    return jax.shard_map(
        functools.partial(body, mesh.shape["slide"], mesh.shape["tile"]),
        mesh=mesh,
        in_specs=placed,
        out_specs=(P(), P(), P(), P(), P()),
        check_vma=False,
    )
```
